32 devices in a mesh: seq: 8 (over z, y), head: 4 (over x, core).
Axes of the slice: x: 2, y: 2, z: 4, core: 2. Of those that a mesh axis runs over, the one named last changes fastest.
Arguments:
- mel_buffer: bfloat16 [16384, 128], P('seq'), may hold values from -6 to 6
- segment_frames: int32 [64], P('seq'), may hold values from 0 to 2048, as said below
- conv1_weight: bfloat16 [3, 128, 1280], replicated, may hold values from -0.3125 to 0.3125
- conv1_bias: float32 [1280], replicated, may hold values from -3 to 3
- conv2_weight: bfloat16 [3, 1280, 1280], P(None, 'seq', 'head'), may hold values from -0.09375 to 0.09375
- conv2_bias: float32 [1280], P('head'), may hold values from -3 to 3
- norm_gain: float32 [1280], replicated, may hold values from 0.1 to 1.9
- norm_bias: float32 [1280], replicated, may hold values from -3 to 3
- qkv_weight: bfloat16 [1280, 3840], P('seq', 'head'), may hold values from -0.15625 to 0.15625
Outputs:
- qkv: bfloat16 [4096, 3840], P('seq', 'head')
The draws below stay inside these ranges and needn't reach their ends.
Inputs may be any that keep to these rules, and one draw needn't show every extreme that they name: `segment_frames`: with S_i the sum of the counts of blocks 0 to i, S_i - (i + 1) * 1024 lies in 0 to 1024 and is 0 for the last block; the counts of one block add to at most 2048, and those of some block add to exactly 2048, all of them in one segment of that block, its other segments being empty.
All inputs are finite; a program needn't handle non-finite values.
Results may differ from the reference program's by a relative error of at most 0.006.
Values may be sent and summed in bfloat16 or wider, within the bound.
A program may use at most 128 MiB of HBM per device.

```python
import math
import jax
import jax.numpy as jnp
from jax import lax

WIDTH = 1280
MELS = 128
CONTEXT = 1500
SEGMENTS = 8
FRAMES_DEV = 1024
BUFFER = 2048
TOK_DEV = 512
FRAMES = 8192
TOKENS = 4096
QKV_WIDTH = 3840
N_SEQ = 8


def draw_segment_frames(key, part):
    key_drift = jax.random.fold_in(key, 11)
    key_pick = jax.random.fold_in(key, 12)
    key_cuts = jax.random.fold_in(key, 13)
    device_ids = jnp.arange(N_SEQ, dtype=jnp.int32)
    displaced = jax.random.randint(key_drift, (N_SEQ,), 0, FRAMES_DEV + 1, dtype=jnp.int32)
    chosen = jax.random.randint(key_pick, (), 1, N_SEQ - 1, dtype=jnp.int32)
    displaced = jnp.where(device_ids == chosen, FRAMES_DEV, displaced)
    displaced = jnp.where(device_ids == chosen - 1, 0, displaced)
    displaced = jnp.where(device_ids == N_SEQ - 1, 0, displaced)
    earlier = jnp.concatenate([jnp.zeros((1,), jnp.int32), displaced[:-1]])
    counts = (FRAMES_DEV + displaced - earlier).astype(jnp.int32)
    raw_cuts = jax.random.randint(key_cuts, (N_SEQ, SEGMENTS - 1), 0, 65536, dtype=jnp.int32)
    cut_rows = raw_cuts * (counts[:, None] + 1) // 65536
    cut_rows = jnp.where((device_ids == chosen)[:, None], 0, cut_rows).astype(jnp.int32)
    cut_rows = jnp.sort(cut_rows, axis=1)
    edges = jnp.concatenate([jnp.zeros((N_SEQ, 1), jnp.int32), cut_rows, counts[:, None]], axis=1)
    return (edges[:, 1:] - edges[:, :-1]).reshape(-1).astype(jnp.int32)


def levels(key, dims, pieces, least, high):
    def one(position, shards_of):
        heights = jax.random.uniform(jax.random.fold_in(jax.random.fold_in(key, 6), position), (shards_of,), jnp.float32, least / len(pieces), high / len(pieces))
        return jnp.repeat(jnp.exp(heights), dims[position] // shards_of).reshape((-1,) + (1,) * (len(dims) - position - 1))

    factor_of = one(*pieces[0])
    for cut in pieces[1:]:
        factor_of = factor_of * one(*cut)
    return factor_of


def noise(own_key, extent, scale, bound, cuts=(), kind=jnp.bfloat16):
    values = scale * jax.random.normal(own_key, extent, jnp.float32)
    if cuts:
        values = values * levels(own_key, extent, cuts, -0.22, 0.18)
    return jnp.clip(values, -bound, bound).astype(kind)


def setup_inputs(seed: int = 0) -> dict:
    arg_keys = jax.random.split(jax.random.key(seed), 10)
    mel_buffer = noise(arg_keys[0], (N_SEQ * BUFFER, MELS), 1.0, 6.0, ((0, 8),))
    segment_frames = draw_segment_frames(jax.random.fold_in(arg_keys[9], 71), 0)
    conv1_weight = noise(arg_keys[2], (3, MELS, WIDTH), (3 * MELS) ** -0.5, 0.3125)
    conv1_bias = noise(arg_keys[3], (WIDTH,), 0.5, 3.0, (), jnp.float32)
    conv2_weight = noise(arg_keys[4], (3, WIDTH, WIDTH), (3 * WIDTH) ** -0.5, 0.09375, ((1, 8), (2, 4)))
    conv2_bias = noise(arg_keys[5], (WIDTH,), 0.5, 3.0, ((0, 4),), jnp.float32)
    norm_gain = jnp.clip(1.0 + 0.18 * jax.random.normal(arg_keys[6], (WIDTH,), jnp.float32), 0.1, 1.9)
    norm_bias = noise(arg_keys[7], (WIDTH,), 0.5, 3.0, (), jnp.float32)
    qkv_weight = noise(arg_keys[8], (WIDTH, QKV_WIDTH), WIDTH ** -0.5, 0.15625, ((0, 8), (1, 4)))
    return dict(mel_buffer=mel_buffer, segment_frames=segment_frames, conv1_weight=conv1_weight, conv1_bias=conv1_bias, conv2_weight=conv2_weight, conv2_bias=conv2_bias, norm_gain=norm_gain, norm_bias=norm_bias, qkv_weight=qkv_weight)


LOG_SCALE = math.log(10000.0)

def sinusoid(token_ids, channel_ids, width_all):
    half_width = width_all // 2
    inv_rate = jnp.exp(-(LOG_SCALE / (half_width - 1)) * (channel_ids % half_width).astype(jnp.float32))
    angles = (token_ids % CONTEXT).astype(jnp.float32)[:, None] * inv_rate[None, :]
    return jnp.where(channel_ids[None, :] < half_width, jnp.sin(angles), jnp.cos(angles))

def layer_norm(values, gain, shift):
    widened = values.astype(jnp.float32)
    average = lax.optimization_barrier(jnp.mean(widened, axis=-1, keepdims=True))
    centered = widened - average
    spread = lax.optimization_barrier(jnp.mean(centered * centered, axis=-1, keepdims=True))
    return (centered * lax.rsqrt(spread + 1e-05) * gain + shift).astype(jnp.bfloat16)

def reference(mel_buffer, segment_frames, conv1_weight, conv1_bias, conv2_weight, conv2_bias, norm_gain, norm_bias, qkv_weight):
    counts = lax.optimization_barrier(jnp.sum(segment_frames.reshape(N_SEQ, SEGMENTS), axis=1)).astype(jnp.int32)
    starts = (jnp.cumsum(counts) - counts).astype(jnp.int32)
    row_ids = jnp.arange(BUFFER, dtype=jnp.int32)
    target = starts[:, None] + row_ids[None, :]
    target = jnp.where(row_ids[None, :] < counts[:, None], target, FRAMES).astype(jnp.int32)
    stream = jnp.zeros((FRAMES + 1, MELS), jnp.bfloat16).at[target.reshape(-1)].set(mel_buffer)[:FRAMES]
    padded = jnp.pad(stream, ((2, 1), (0, 0)))
    channel = jnp.arange(WIDTH, dtype=jnp.int32)

    def one_block(block_index):
        offset = (block_index * FRAMES_DEV).astype(jnp.int32)
        window = lax.dynamic_slice_in_dim(padded, offset, FRAMES_DEV + 3, 0)
        running = jnp.zeros((FRAMES_DEV + 1, WIDTH), jnp.float32)
        for k in range(3):
            running = running + jnp.dot(window[k:k + FRAMES_DEV + 1], conv1_weight[k], preferred_element_type=jnp.float32)
        first_layer = jax.nn.gelu(running + conv1_bias, approximate=False).astype(jnp.bfloat16)
        frame_ids = offset - 1 + jnp.arange(FRAMES_DEV + 1, dtype=jnp.int32)
        first_layer = jnp.where((frame_ids >= 0)[:, None], first_layer, jnp.zeros_like(first_layer))
        frame_pairs = first_layer[:FRAMES_DEV].reshape(TOK_DEV, 2, WIDTH)
        later_pairs = first_layer[1:].reshape(TOK_DEV, 2, WIDTH)
        conv_taps = (frame_pairs[:, 0], frame_pairs[:, 1], later_pairs[:, 1])
        stem_sum = jnp.zeros((TOK_DEV, WIDTH), jnp.float32)
        for k in range(3):
            stem_sum = stem_sum + jnp.dot(conv_taps[k], conv2_weight[k], preferred_element_type=jnp.float32)
        token_ids = (block_index * TOK_DEV).astype(jnp.int32) + jnp.arange(TOK_DEV, dtype=jnp.int32)
        stem = (jax.nn.gelu(stem_sum + conv2_bias, approximate=False) + sinusoid(token_ids, channel, WIDTH)).astype(jnp.bfloat16)
        normed = layer_norm(stem, norm_gain, norm_bias)
        return jnp.dot(normed, qkv_weight, preferred_element_type=jnp.float32).astype(jnp.bfloat16)
    blocks = lax.map(one_block, jnp.arange(N_SEQ, dtype=jnp.int32))
    return blocks.reshape(TOKENS, QKV_WIDTH)
```

```python
import functools
import math

import jax
import jax.numpy as jnp
from jax import lax
from jax.experimental import pallas as pl
from jax.experimental.pallas import tpu as pltpu
from jax.sharding import PartitionSpec as P

CONTEXT = 1500


LOG_SCALE = math.log(10000.0)


def prefix(value, axis, join, neutral):
    count, mine = (lax.axis_size(axis), lax.axis_index(axis))
    pieces = lax.all_gather(value, axis)
    running = jnp.full_like(value, 0) + jnp.asarray(neutral, value.dtype)

    def step(position, running):
        longer = join(running, pieces[position])
        return jnp.where(position < mine, longer, running)

    return lax.fori_loop(0, count - 1, step, running)


def from_behind(value, axis, by):
    size = lax.axis_size(axis)
    pairs = [(i, i + by) for i in range(size) if 0 <= i + by < size]
    return lax.ppermute(value, axis, pairs)


def padded(value, sides, width):
    for axis, dim in sides:
        size, length = (lax.axis_size(axis), value.shape[dim])
        up = [(i, (i + 1) % size) for i in range(size - 1)]
        down = [(j, i) for i, j in up]
        last = lax.slice_in_dim(value, length - width, length, axis=dim)
        initial = lax.slice_in_dim(value, 0, width, axis=dim)
        before = lax.ppermute(last, axis, up)
        after = lax.ppermute(initial, axis, down)
        value = jnp.concatenate([before, value, after], axis=dim)
    return value


def sinusoid(token_ids, channel_ids, width_all):
    half_width = width_all // 2
    inv_rate = jnp.exp(
        -(LOG_SCALE / (half_width - 1)) * (channel_ids % half_width).astype(jnp.float32)
    )
    angles = (token_ids % CONTEXT).astype(jnp.float32)[:, None] * inv_rate[None, :]
    return jnp.where(channel_ids[None, :] < half_width, jnp.sin(angles), jnp.cos(angles))


def layer_norm(values, gain, shift):
    widened = values.astype(jnp.float32)
    average = jnp.mean(widened, axis=-1, keepdims=True)
    centered = widened - average
    spread = jnp.mean(centered * centered, axis=-1, keepdims=True)
    return (centered * lax.rsqrt(spread + 1e-05) * gain + shift).astype(jnp.bfloat16)


def add_sum(left, right):
    return left + right


def project_rows(normed, shard_rows):
    return jnp.dot(normed, shard_rows, preferred_element_type=jnp.float32)


def per_device(
    mel_buffer,
    segment_frames,
    conv1_weight,
    conv1_bias,
    conv2_weight,
    conv2_bias,
    norm_gain,
    norm_bias,
    qkv_weight,
):
    frames_dev = mel_buffer.shape[0] // 2
    tok_rows = frames_dev // 2
    width_all = conv1_weight.shape[2]
    seq_place = lax.axis_index("seq")
    head_place = lax.axis_index("head")
    own_count = jnp.sum(segment_frames)
    start_frame = prefix(own_count, "seq", add_sum, jnp.zeros((), jnp.int32))
    displaced = (start_frame - seq_place * frames_dev).astype(jnp.int32)
    tail_rows = lax.dynamic_slice_in_dim(mel_buffer, frames_dev - displaced, frames_dev, 0)
    arrived = from_behind(tail_rows, "seq", 1)
    front_pad = jnp.concatenate([jnp.zeros_like(arrived), mel_buffer[:frames_dev]], axis=0)
    own_rows = lax.dynamic_slice_in_dim(front_pad, frames_dev - displaced, frames_dev, 0)
    row_ids = jnp.arange(frames_dev, dtype=jnp.int32)
    frames = jnp.where((row_ids < displaced)[:, None], arrived, own_rows)
    rimmed = padded(frames, (("seq", 0),), 2)
    running = jnp.zeros((frames_dev + 1, width_all), jnp.float32)
    for k in range(3):
        running = running + jnp.dot(
            rimmed[k : k + frames_dev + 1], conv1_weight[k], preferred_element_type=jnp.float32
        )
    first_layer = jax.nn.gelu(running + conv1_bias, approximate=False).astype(jnp.bfloat16)
    keep_mask = (jnp.arange(frames_dev + 1, dtype=jnp.int32) > 0) | (seq_place > 0)
    first_layer = jnp.where(keep_mask[:, None], first_layer, jnp.zeros_like(first_layer))
    frame_pairs = first_layer[:frames_dev].reshape(tok_rows, 2, width_all)
    later_pairs = first_layer[1:].reshape(tok_rows, 2, width_all)
    conv_taps = (frame_pairs[:, 0], frame_pairs[:, 1], later_pairs[:, 1])
    quarter_width = conv2_weight.shape[2]
    zero_start = jnp.zeros((tok_rows, quarter_width), jnp.float32)
    stem_sum = zero_start
    shard_rows = lax.all_gather(conv2_weight, "seq", axis=1, tiled=True)
    for k in range(3):
        inputs = conv_taps[k]
        stem_sum = stem_sum + jnp.dot(inputs, shard_rows[k], preferred_element_type=jnp.float32)
    token_ids = seq_place * tok_rows + jnp.arange(tok_rows, dtype=jnp.int32)
    channel = head_place * quarter_width + jnp.arange(quarter_width, dtype=jnp.int32)
    features = (
        jax.nn.gelu(stem_sum + conv2_bias, approximate=False)
        + sinusoid(token_ids, channel, width_all)
    ).astype(jnp.bfloat16)
    quarter = lax.all_to_all(features, "head", split_axis=0, concat_axis=1, tiled=True)
    normed = layer_norm(quarter, norm_gain, norm_bias)
    widened_rows = lax.all_gather(qkv_weight, "head", axis=1, tiled=True)
    qkv_part = project_rows(normed, lax.all_gather(widened_rows, "seq", axis=0, tiled=True))
    return lax.all_to_all(
        qkv_part.astype(jnp.bfloat16), "head", split_axis=1, concat_axis=0, tiled=True
    )


MESH = pl.DeviceIdType.MESH
HALO = 16
ROWS = 128
W2_PIECES = (2, 0, 1, 5)
WQ_PIECES = (3, 4, 6)


def gelu(v):
    return 0.5 * v * (1.0 + lax.erf(v * math.sqrt(0.5)))


def fused_kernel(
    dims, vec_ref, mel_ref, w1_ref, w2_ref, wq_ref,
    out_ref, seg_all, tail_send, tail_recv, fr, frp, halo_prev, halo_next, ebuf, obuf, x_even, x_odd,
    w1h, b1h, f_mid, f_odd, w2g, wqg, rest, restg, restq, restqg, acc0, accp, psend, precv, place,
    stem, gperm, nrm, seg_s, seg_r, tail_s, tail_r, fr_s, fr_r, halo_s, halo_r,
    w_s, w_r, loc, p_s, p_r, st_s, st_r,
):
    n, depth, width_all, quarter = dims
    nz = n // 2
    toks = fr.shape[1]
    frames_dev = 2 * toks
    plane = 2 * toks
    half_width = width_all // 2
    chunks = toks // ROWS
    me = lax.axis_index("seq")
    h = lax.axis_index("head")
    z, y = me // 2, me % 2
    partner = z * 2 + (1 - y)
    f32, bf16 = jnp.float32, jnp.bfloat16
    core = h % 2
    core_peer = (h // 2) * 2 + (1 - core)
    x_peer = lax.rem(h + 2, 4)
    far = lax.rem(core_peer + 2, 4)
    seg_ref = vec_ref.at[pl.ds(8, 8), pl.ds(0, 128)]
    pending = []

    def remote(src, dst, ss, rs, axis, peer):
        return pltpu.make_async_remote_copy(
            src_ref=src, dst_ref=dst, send_sem=ss, recv_sem=rs,
            device_id={axis: peer}, device_id_type=MESH,
        )

    def start(cond, copy):
        if cond is None:
            copy.start()
        else:
            pl.when(cond)(copy.start)
        pending.append((cond, copy))

    def both(a, b):
        if a is None:
            return b
        return a if b is None else jnp.logical_and(a, b)

    barrier = pltpu.get_barrier_semaphore()
    for p in range(1, n):
        pl.semaphore_signal(
            barrier, inc=1, device_id={"seq": lax.rem(me + p, n)}, device_id_type=MESH
        )
    for p in range(1, 4):
        pl.semaphore_signal(
            barrier, inc=1, device_id={"head": lax.rem(h + p, 4)}, device_id_type=MESH
        )
    pl.semaphore_wait(barrier, n - 1 + 3)

    for p in range(1, n):
        dst = lax.rem(me + p, n)
        start(None, remote(seg_ref, seg_all.at[me], seg_s.at[p], seg_r.at[me], "seq", dst))

    half = depth // 2
    out_cols = wqg.shape[1]
    main2, main_q = quarter - 64, out_cols - 64
    head_rows = 2 * depth - 64
    first_q = head_rows - depth
    lanes2, lanes_q = pl.ds(0, main2), pl.ds(0, main_q)
    rest_base = 4 * head_rows

    def row_first(s):
        return (s // 2) * head_rows + (s % 2) * depth

    def row_last(s):
        even = (s // 2) * head_rows + first_q
        odd = rest_base + (s // 2) * 64
        return (1 - s % 2) * even + (s % 2) * odd

    def gathered(p, s):
        if p < 3:
            return w2g.at[pl.ds(pl.multiple_of(p * half_width + (s // 2) * depth, 32), depth), lanes2]
        if p == 5:
            return restg.at[s // 2]
        if p == 6:
            return restqg.at[s]
        if p == 3:
            return wqg.at[pl.ds(pl.multiple_of(row_first(s), 32), first_q), lanes_q]
        return wqg.at[pl.ds(pl.multiple_of(row_last(s), 32), 64), lanes_q]

    def own(p):
        if p < 3:
            return w2_ref.at[p, :, lanes2]
        if p == 5:
            return rest
        if p == 6:
            return restq
        return wq_ref.at[pl.ds(0, first_q) if p == 3 else pl.ds(first_q, 64), lanes_q]

    has_up, has_down = z < nz - 1, z > 0

    def push(cond, p, s, way, mine=False):
        peer = (lax.rem(me + 2, n), lax.rem(me + n - 2, n), partner)[way]
        src = own(p) if mine else gathered(p, s)
        start(cond, remote(src, gathered(p, s), w_s.at[p, s, way], w_r.at[p, s], "seq", peer))

    def arrive(cond, p, s):
        copy = remote(gathered(p, s), gathered(p, s), w_s.at[p, s, 0], w_r.at[p, s], "seq", partner)
        if cond is None:
            copy.wait_recv()
        else:
            pl.when(cond)(copy.wait_recv)

    def own_along_z(p):
        push(has_up, p, me, 0, True)
        push(has_down, p, me, 1, True)

    def own_local(p):
        return pltpu.make_async_copy(own(p), gathered(p, me), loc.at[p])

    def source(k, way):
        valid = z - k >= 0 if way == 0 else z + k <= nz - 1
        onward = has_up if way == 0 else has_down
        s = lax.rem(me + (-2 * k if way == 0 else 2 * k) + 2 * n, n)
        return valid, onward, s

    def relay(p, k):
        for way in (0, 1):
            valid, onward, s = source(k, way)
            arrive(valid, p, s)
            push(both(valid, onward), p, s, way)

    def relay_z(p, k):
        for way in (0, 1):
            valid, onward, s = source(k, way)
            arrive(both(valid, onward), p, s)
            push(both(valid, onward), p, s, way)

    def relay_y(p, k):
        for way in (0, 1):
            valid, onward, s = source(k, way)
            arrive(both(valid, jnp.logical_not(onward)), p, s)
            push(valid, p, s, 2)

    own_along_z(2)
    own_along_z(0)
    restq[:, 0:64] = wq_ref[0:half, main_q:]
    restq[:, 64:128] = wq_ref[half:, main_q:]
    rest[0:depth, 0:64] = w2_ref[0, :, main2:]
    rest[0:depth, 64:128] = w2_ref[1, :, main2:]
    rest[depth:, 0:64] = w2_ref[2, 0:half, main2:]
    rest[depth:, 64:128] = w2_ref[2, half:, main2:]
    for p in W2_PIECES + WQ_PIECES:
        own_local(p).start()

    total = jnp.zeros((8, 128), f32)
    for p in range(1, n):
        src = lax.rem(me + n - p, n)
        remote(seg_ref, seg_all.at[src], seg_s.at[p], seg_r.at[src], "seq", src).wait_recv()
        total = total + jnp.where(src < me, seg_all[src], 0.0)
    total = jnp.sum(jnp.sum(total, axis=1, keepdims=True), axis=0, keepdims=True)
    moved = total.astype(jnp.int32) - me * frames_dev

    rows = ROWS

    def shifted(first, parity, depth_rows):
        frame = 2 * (first + lax.broadcasted_iota(jnp.int32, (rows, depth_rows), 0)) + parity
        column = lax.broadcasted_iota(jnp.int32, (rows, depth_rows), 1)
        pick = jnp.where(frame - column == moved, 1.0, 0.0).astype(bf16)
        return jnp.dot(pick, mel_ref[:depth_rows, :], preferred_element_type=f32)

    def tail_step(i, c):
        at = pl.multiple_of(i * rows, rows)
        tail_send[pl.ds(at, rows), :] = shifted(toks + at, core, 2 * frames_dev).astype(bf16)
        return c

    lax.fori_loop(0, toks // rows, tail_step, 0)
    tail = remote(tail_send, tail_recv.at[core], tail_s.at[0], tail_r.at[core],
                  "seq", lax.rem(me + 1, n))
    start(me < n - 1, tail)
    own_along_z(1)
    own_along_z(5)

    base = pl.multiple_of(HALO + y * toks, 16)
    other = pl.multiple_of(HALO + (1 - y) * toks, 16)
    for parity, buf in ((0, ebuf), (1, obuf)):
        def own_step(i, c):
            at = pl.multiple_of(i * rows, rows)
            buf[pl.ds(base + at, rows), :] = shifted(at, parity, frames_dev)
            return c
        lax.fori_loop(0, toks // rows, own_step, 0)
    for p in W2_PIECES[:2]:
        relay(p, 1)

    pl.when(me > 0)(tail.wait_recv)
    start(me > 0, remote(tail_recv.at[core], tail_recv.at[core], tail_s.at[1], tail_r.at[core],
                         "head", core_peer))
    pl.when(me > 0)(remote(
        tail_recv.at[1 - core], tail_recv.at[1 - core], tail_s.at[1], tail_r.at[1 - core],
        "head", core_peer).wait_recv)
    for parity, buf in ((0, ebuf), (1, obuf)):
        frame = 2 * lax.broadcasted_iota(jnp.int32, (toks, 128), 0) + parity
        joined = jnp.where(
            frame < moved, tail_recv[parity].astype(f32), buf[pl.ds(base, toks), :])
        buf[pl.ds(base, toks), :] = joined
        fr[parity] = joined.astype(bf16)

    start(None, remote(fr.at[core], frp.at[core], fr_s.at[0], fr_r.at[core], "seq", partner))
    upper, lower = both(y == 1, has_up), both(y == 0, has_down)
    one, two = lax.rem(me + 1, n), lax.rem(me + 2, n)
    back, back2 = lax.rem(me + n - 1, n), lax.rem(me + n - 2, n)
    tail_rows, head_part = pl.ds(toks - HALO, HALO), pl.ds(0, HALO)
    for i, peer in enumerate((one, two)):
        for parity in (0, 1):
            start(upper, remote(fr.at[parity, tail_rows, :], halo_prev.at[parity],
                                halo_s.at[2 * i + parity], halo_r.at[parity], "seq", peer))
    for i, peer in enumerate((back, back2)):
        start(lower, remote(fr.at[0, head_part, :], halo_next,
                            halo_s.at[4 + i], halo_r.at[2], "seq", peer))
    for p in WQ_PIECES:
        push(None, p, me, 2, True)
    for p in W2_PIECES[2:]:
        relay(p, 1)

    for yy in (0, 1):
        @pl.when(y == yy)
        def _():
            for q in range(nz):
                dst = slice(q * depth, (q + 1) * depth)
                src = slice((2 * q + yy) * depth, (2 * q + yy + 1) * depth)
                w1h[:, dst] = w1_ref[:, src]
                b1h[0:1, dst] = vec_ref[0:1, src]
    for j in range(4):
        a, b = j * quarter, j * quarter + main2
        for r in (0, 1):
            gperm[r : r + 1, j * main2 : (j + 1) * main2] = vec_ref[1 + r : 2 + r, a:b]
            gperm[r : r + 1, rest_base + j * 64 : rest_base + (j + 1) * 64] = (
                vec_ref[1 + r : 2 + r, b : b + 64])

    first_token = lax.rem(me * toks, CONTEXT)
    lane = lax.broadcasted_iota(jnp.int32, (1, main2), 1)
    first_channel = lax.rem(h * quarter, half_width)

    def rate_of(channel):
        return jnp.exp(-(LOG_SCALE / (half_width - 1)) * (channel + first_channel).astype(f32))

    rate_main, rate_rest = rate_of(lane), rate_of(main2 + lax.rem(lane, 64))
    packed = ROWS + ROWS // 4

    def fill_place(wave):
        def step(i, c):
            token = first_token + i * ROWS + lax.broadcasted_iota(jnp.int32, (ROWS, 1), 0)
            token = jnp.where(token >= CONTEXT, token - CONTEXT, token)
            place[i, 0:ROWS, :] = wave(token.astype(f32) * rate_main)
            shape = (ROWS // 4, main2)
            token = (first_token + i * ROWS + lax.broadcasted_iota(jnp.int32, shape, 0)
                     + (ROWS // 4) * (lax.broadcasted_iota(jnp.int32, shape, 1) // 64))
            token = jnp.where(token >= CONTEXT, token - CONTEXT, token)
            place[i, ROWS:packed, :] = wave(token.astype(f32) * rate_rest)
            return c
        lax.fori_loop(0, chunks, step, 0)

    pl.when(h < 2)(lambda: fill_place(jnp.sin))
    pl.when(h >= 2)(lambda: fill_place(jnp.cos))

    for p in W2_PIECES[:2]:
        relay(p, 2)

    remote(fr.at[core], frp.at[core], fr_s.at[0], fr_r.at[core], "seq", partner).wait_recv()
    start(None, remote(frp.at[core], frp.at[core], fr_s.at[1], fr_r.at[core], "head", core_peer))
    remote(frp.at[1 - core], frp.at[1 - core], fr_s.at[1], fr_r.at[1 - core],
           "head", core_peer).wait_recv()
    for i in (0, 1):
        pl.when(has_down)(remote(halo_prev.at[i], halo_prev.at[i], halo_s.at[i], halo_r.at[i],
                                 "seq", partner).wait_recv)
    pl.when(has_up)(remote(halo_next, halo_next, halo_s.at[4], halo_r.at[2],
                           "seq", partner).wait_recv)
    ebuf[pl.ds(other, toks), :] = frp[0].astype(f32)
    obuf[pl.ds(other, toks), :] = frp[1].astype(f32)
    ebuf[0:HALO, :] = jnp.where(z > 0, halo_prev[0].astype(f32), 0.0)
    obuf[0:HALO, :] = jnp.where(z > 0, halo_prev[1].astype(f32), 0.0)
    ebuf[HALO + plane :, :] = jnp.where(z < nz - 1, halo_next[...].astype(f32), 0.0)
    x_even[:, 0:128] = obuf[HALO - 1 : HALO - 1 + plane, :].astype(bf16)
    x_even[:, 128:256] = ebuf[HALO : HALO + plane, :].astype(bf16)
    x_even[:, 256:384] = obuf[HALO : HALO + plane, :].astype(bf16)
    x_odd[:, 0:128] = ebuf[0 : HALO + plane, :].astype(bf16)
    x_odd[:, 128:256] = obuf[0 : HALO + plane, :].astype(bf16)
    x_odd[:, 256:384] = ebuf[1 : HALO + plane + 1, :].astype(bf16)

    tiles = [(a, min(a + 256, half_width)) for a in range(0, half_width, 256)]

    def first_conv(inputs, a, b):
        acc = jnp.dot(inputs, w1h[:, a:b], preferred_element_type=f32)
        return gelu(acc + b1h[0:1, a:b]).astype(bf16)

    def even_step(i, c):
        at = pl.ds(pl.multiple_of(i * toks, 16), toks)
        for a, b in tiles:
            f_mid[at, a:b] = first_conv(x_even[at, :], a, b)
        return c

    def odd_step(i, c):
        at = pl.multiple_of(i * toks, 16)
        for a, b in tiles:
            value = first_conv(x_odd[pl.ds(HALO + at, toks), :], a, b)
            f_mid[pl.ds(at, toks), half_width + a : half_width + b] = value
            f_odd[pl.ds(HALO + at, toks), a:b] = value
        return c

    lax.fori_loop(0, 2, even_step, 0)
    for p in W2_PIECES[2:]:
        relay(p, 2)
    for p in WQ_PIECES:
        own_along_z(p)
    lax.fori_loop(0, 2, odd_step, 0)
    for a, b in tiles:
        early = first_conv(x_odd[0:HALO, :], a, b)
        f_odd[0:HALO, a:b] = jnp.where(z > 0, early.astype(f32), 0.0).astype(bf16)
    for p in WQ_PIECES:
        relay_z(p, 1)

    for p in W2_PIECES:
        relay(p, 3)
    for p in W2_PIECES + WQ_PIECES:
        own_local(p).wait()
    for q in range(nz):
        for tap in (0, 1):
            at = tap * half_width + q * depth
            w2g[at : at + depth, main2:] = restg[q, 0:depth, 64 * tap : 64 * tap + 64]
        at = 2 * half_width + q * depth
        w2g[at : at + half, main2:] = restg[q, depth:, 0:64]
        w2g[at + half : at + depth, main2:] = restg[q, depth:, 64:128]

    odd_rows = (HALO + toks) // 3

    def partial_sums(slab, store):
        def tap_zero(i, c):
            at = pl.multiple_of(i * odd_rows, 16)
            acc0[pl.ds(at, odd_rows), :] = jnp.dot(
                f_odd[pl.ds(pl.multiple_of(slab * toks + at, 16), odd_rows), :],
                w2g[0:half_width, :], preferred_element_type=f32)
            return c

        lax.fori_loop(0, 3, tap_zero, 0)
        for i in range(chunks):
            at = pl.multiple_of(slab * toks + i * ROWS, ROWS)
            acc = jnp.dot(f_mid[pl.ds(at, ROWS), :], w2g[half_width:, :], preferred_element_type=f32)
            acc = acc + acc0[HALO - 1 + i * ROWS : HALO - 1 + (i + 1) * ROWS, :]
            store(i, acc)

    def store_packed(ref, i, acc):
        acc = acc.astype(ref.dtype)
        ref[i, 0:ROWS, :] = acc[:, 0:main2]
        step = ROWS // 4
        for b in range(4):
            ref[i, ROWS:packed, 64 * b : 64 * b + 64] = acc[b * step : (b + 1) * step, main2:]

    def send_partial(i, acc):
        store_packed(psend, i, acc)
        start(None, remote(psend.at[i], precv.at[i], p_s.at[i], p_r.at[i], "seq", partner))

    partial_sums(1 - y, send_partial)
    for p in WQ_PIECES:
        relay_z(p, 2)
    partial_sums(y, lambda i, acc: store_packed(accp, i, acc))

    bias_main = vec_ref[3:4, 0:main2]
    bias_rest = jnp.concatenate([vec_ref[3:4, main2:quarter]] * 4, axis=1)
    for i in range(chunks):
        remote(psend.at[i], precv.at[i], p_s.at[i], p_r.at[i], "seq", partner).wait_recv()
        for part, bias in ((slice(0, ROWS), bias_main), (slice(ROWS, packed), bias_rest)):
            value = accp[i, part, :] + precv[i, part, :].astype(f32) + bias
            stem[h, i, part, :] = (gelu(value) + place[i, part, :]).astype(bf16)
        mine = stem.at[h, i]
        start(None, remote(mine, mine, st_s.at[0, i], st_r.at[0, i], "head", x_peer))
        start(None, remote(mine, mine, st_s.at[1, i], st_r.at[1, i], "head", core_peer))

    for p in WQ_PIECES:
        relay_y(p, 1)
    for i in range(chunks):
        got = stem.at[x_peer, i]
        remote(got, got, st_s.at[0, i], st_r.at[0, i], "head", x_peer).wait_recv()
        start(None, remote(got, got, st_s.at[2, i], st_r.at[2, i], "head", core_peer))
    for i in range(chunks):
        got = stem.at[core_peer, i]
        remote(got, got, st_s.at[1, i], st_r.at[1, i], "head", core_peer).wait_recv()
        got = stem.at[far, i]
        remote(got, got, st_s.at[2, i], st_r.at[2, i], "head", core_peer).wait_recv()

    def normalise(i, c):
        step = ROWS // 4
        parts = [stem[j, i, 0:ROWS, :].astype(f32) for j in range(4)]
        tails = [stem[j, i, ROWS:packed, :].astype(f32) for j in range(4)]
        parts.append(jnp.concatenate(
            [jnp.concatenate([t[:, 64 * b : 64 * b + 64] for t in tails], axis=1) for b in range(4)],
            axis=0))
        mean = jnp.sum(sum(parts), axis=1, keepdims=True) / width_all
        parts = [v - mean for v in parts]
        var = jnp.sum(sum(v * v for v in parts), axis=1, keepdims=True) / width_all
        scale = lax.rsqrt(var + 1e-05)
        at = pl.ds(pl.multiple_of(i * ROWS, ROWS), ROWS)
        for j, v in enumerate(parts):
            lanes = slice(j * main2, (j + 1) * main2)
            nrm[at, lanes] = (v * scale * gperm[0:1, lanes] + gperm[1:2, lanes]).astype(bf16)
        return c

    lax.fori_loop(0, chunks, normalise, 0)
    for k in (2, 3):
        for p in WQ_PIECES:
            relay_y(p, k)
    for p in WQ_PIECES:
        for q in range(nz):
            arrive(None, p, 2 * q + (1 - y))
    for s in range(n):
        lo, hi = row_first(s), row_last(s)
        wqg[lo : lo + half, main_q:] = restqg[s, :, 0:64]
        wqg[lo + half : lo + first_q, main_q:] = restqg[s, 0 : first_q - half, 64:128]
        wqg[hi : hi + 64, main_q:] = restqg[s, first_q - half :, 64:128]

    def project(i, c):
        at = pl.ds(pl.multiple_of(i * 256, 256), 256)
        for a in range(0, out_cols, 256):
            b = min(a + 256, out_cols)
            out_ref[at, a:b] = jnp.dot(
                nrm[at, :], wqg[:, a:b], preferred_element_type=f32).astype(bf16)
        return c

    lax.fori_loop(0, toks // 256, project, 0)

    for cond, copy in pending:
        if cond is None:
            copy.wait_send()
        else:
            pl.when(cond)(copy.wait_send)


def fused_device(
    n, mel_buffer, segment_frames, conv1_weight, conv1_bias, conv2_weight, conv2_bias,
    norm_gain, norm_bias, qkv_weight,
):
    toks = mel_buffer.shape[0] // 4
    taps, mels, width_all = conv1_weight.shape
    depth, quarter = conv2_weight.shape[1:]
    out_cols = qkv_weight.shape[1]
    bf16, f32 = jnp.bfloat16, jnp.float32
    vec = jnp.zeros((), f32)
    rows_of = (conv1_bias, norm_gain, norm_bias, conv2_bias), (segment_frames.astype(f32),)
    for first, group in zip((0, 8), rows_of):
        for j, row in enumerate(group):
            vec = vec + jnp.pad(row[None, :], ((first + j, 15 - first - j), (0, width_all - row.shape[0])))
    vmem = pl.BlockSpec(memory_space=pltpu.VMEM)
    dma = pltpu.SemaphoreType.DMA
    plane, inner = 2 * toks, width_all // 2
    chunks, packed, main2 = toks // ROWS, ROWS + ROWS // 4, quarter - 64
    return pl.pallas_call(
        functools.partial(fused_kernel, (n, depth, width_all, quarter)),
        out_shape=jax.ShapeDtypeStruct((toks, out_cols), bf16),
        in_specs=[vmem] * 5,
        out_specs=vmem,
        scratch_shapes=[
            pltpu.VMEM((n, 8, 128), f32),
            pltpu.VMEM((toks, 128), bf16),
            pltpu.VMEM((2, toks, 128), bf16),
            pltpu.VMEM((2, toks, 128), bf16),
            pltpu.VMEM((2, toks, 128), bf16),
            pltpu.VMEM((2, HALO, 128), bf16),
            pltpu.VMEM((HALO, 128), bf16),
            pltpu.VMEM((plane + 2 * HALO, 128), f32),
            pltpu.VMEM((plane + 2 * HALO, 128), f32),
            pltpu.VMEM((plane, 384), bf16),
            pltpu.VMEM((plane + HALO, 384), bf16),
            pltpu.VMEM((taps * mels, inner), bf16),
            pltpu.VMEM((8, inner), f32),
            pltpu.VMEM((plane, width_all), bf16),
            pltpu.VMEM((plane + HALO, inner), bf16),
            pltpu.VMEM((3 * inner, quarter), bf16),
            pltpu.VMEM((width_all, out_cols), bf16),
            pltpu.VMEM((3 * depth // 2, 128), bf16),
            pltpu.VMEM((n // 2, 3 * depth // 2, 128), bf16),
            pltpu.VMEM((depth // 2, 128), bf16),
            pltpu.VMEM((n, depth // 2, 128), bf16),
            pltpu.VMEM((toks + HALO, quarter), f32),
            pltpu.VMEM((chunks, packed, main2), f32),
            pltpu.VMEM((chunks, packed, main2), bf16),
            pltpu.VMEM((chunks, packed, main2), bf16),
            pltpu.VMEM((chunks, packed, main2), f32),
            pltpu.VMEM((4, chunks, packed, main2), bf16),
            pltpu.VMEM((8, width_all), f32),
            pltpu.VMEM((toks, width_all), bf16),
            dma((n,)), dma((n,)), dma((2,)), dma((2,)), dma((2,)), dma((2,)), dma((6,)), dma((3,)),
            dma((7, n, 3)), dma((7, n)), dma((7,)), dma((chunks,)), dma((chunks,)),
            dma((3, chunks)), dma((3, chunks)),
        ],
        compiler_params=pltpu.CompilerParams(
            collective_id=0, has_side_effects=True, vmem_limit_bytes=60 * 1024 * 1024
        ),
    )(
        vec, mel_buffer, conv1_weight.reshape(taps * mels, width_all), conv2_weight, qkv_weight,
    )


def solution(mesh):
    n_seq, n_head = mesh.shape["seq"], mesh.shape["head"]

    def local(*args):
        depth, quarter = args[4].shape[1:]
        fits = n_head == 4 and n_seq == 8 and depth == 160 and quarter == 320
        if fits and args[0].shape[0] == 2048:
            return fused_device(n_seq, *args)
        return per_device(*args)

    in_specs = (
        P("seq", None),
        P("seq"),
        P(),
        P(),
        P(None, "seq", "head"),
        P("head"),
        P(),
        P(),
        P("seq", "head"),
    )
    out_specs = P("seq", "head")
    return jax.shard_map(
        local, mesh=mesh, in_specs=in_specs, out_specs=out_specs, check_vma=False
    )
```

```python
import functools
import math

import jax
import jax.numpy as jnp
from jax import lax
from jax.experimental import pallas as pl
from jax.experimental.pallas import tpu as pltpu
from jax.sharding import PartitionSpec as P

CONTEXT = 1500


LOG_SCALE = math.log(10000.0)


def prefix(value, axis, join, neutral):
    count, mine = (lax.axis_size(axis), lax.axis_index(axis))
    pieces = lax.all_gather(value, axis)
    running = jnp.full_like(value, 0) + jnp.asarray(neutral, value.dtype)

    def step(position, running):
        longer = join(running, pieces[position])
        return jnp.where(position < mine, longer, running)

    return lax.fori_loop(0, count - 1, step, running)


def from_behind(value, axis, by):
    size = lax.axis_size(axis)
    pairs = [(i, i + by) for i in range(size) if 0 <= i + by < size]
    return lax.ppermute(value, axis, pairs)


def padded(value, sides, width):
    for axis, dim in sides:
        size, length = (lax.axis_size(axis), value.shape[dim])
        up = [(i, (i + 1) % size) for i in range(size - 1)]
        down = [(j, i) for i, j in up]
        last = lax.slice_in_dim(value, length - width, length, axis=dim)
        initial = lax.slice_in_dim(value, 0, width, axis=dim)
        before = lax.ppermute(last, axis, up)
        after = lax.ppermute(initial, axis, down)
        value = jnp.concatenate([before, value, after], axis=dim)
    return value


def sinusoid(token_ids, channel_ids, width_all):
    half_width = width_all // 2
    inv_rate = jnp.exp(
        -(LOG_SCALE / (half_width - 1)) * (channel_ids % half_width).astype(jnp.float32)
    )
    angles = (token_ids % CONTEXT).astype(jnp.float32)[:, None] * inv_rate[None, :]
    return jnp.where(channel_ids[None, :] < half_width, jnp.sin(angles), jnp.cos(angles))


def layer_norm(values, gain, shift):
    widened = values.astype(jnp.float32)
    average = jnp.mean(widened, axis=-1, keepdims=True)
    centered = widened - average
    spread = jnp.mean(centered * centered, axis=-1, keepdims=True)
    return (centered * lax.rsqrt(spread + 1e-05) * gain + shift).astype(jnp.bfloat16)


def add_sum(left, right):
    return left + right


def project_rows(normed, shard_rows):
    return jnp.dot(normed, shard_rows, preferred_element_type=jnp.float32)


def per_device(
    mel_buffer,
    segment_frames,
    conv1_weight,
    conv1_bias,
    conv2_weight,
    conv2_bias,
    norm_gain,
    norm_bias,
    qkv_weight,
):
    frames_dev = mel_buffer.shape[0] // 2
    tok_rows = frames_dev // 2
    width_all = conv1_weight.shape[2]
    seq_place = lax.axis_index("seq")
    head_place = lax.axis_index("head")
    own_count = jnp.sum(segment_frames)
    start_frame = prefix(own_count, "seq", add_sum, jnp.zeros((), jnp.int32))
    displaced = (start_frame - seq_place * frames_dev).astype(jnp.int32)
    tail_rows = lax.dynamic_slice_in_dim(mel_buffer, frames_dev - displaced, frames_dev, 0)
    arrived = from_behind(tail_rows, "seq", 1)
    front_pad = jnp.concatenate([jnp.zeros_like(arrived), mel_buffer[:frames_dev]], axis=0)
    own_rows = lax.dynamic_slice_in_dim(front_pad, frames_dev - displaced, frames_dev, 0)
    row_ids = jnp.arange(frames_dev, dtype=jnp.int32)
    frames = jnp.where((row_ids < displaced)[:, None], arrived, own_rows)
    rimmed = padded(frames, (("seq", 0),), 2)
    running = jnp.zeros((frames_dev + 1, width_all), jnp.float32)
    for k in range(3):
        running = running + jnp.dot(
            rimmed[k : k + frames_dev + 1], conv1_weight[k], preferred_element_type=jnp.float32
        )
    first_layer = jax.nn.gelu(running + conv1_bias, approximate=False).astype(jnp.bfloat16)
    keep_mask = (jnp.arange(frames_dev + 1, dtype=jnp.int32) > 0) | (seq_place > 0)
    first_layer = jnp.where(keep_mask[:, None], first_layer, jnp.zeros_like(first_layer))
    frame_pairs = first_layer[:frames_dev].reshape(tok_rows, 2, width_all)
    later_pairs = first_layer[1:].reshape(tok_rows, 2, width_all)
    conv_taps = (frame_pairs[:, 0], frame_pairs[:, 1], later_pairs[:, 1])
    quarter_width = conv2_weight.shape[2]
    zero_start = jnp.zeros((tok_rows, quarter_width), jnp.float32)
    stem_sum = zero_start
    shard_rows = lax.all_gather(conv2_weight, "seq", axis=1, tiled=True)
    for k in range(3):
        inputs = conv_taps[k]
        stem_sum = stem_sum + jnp.dot(inputs, shard_rows[k], preferred_element_type=jnp.float32)
    token_ids = seq_place * tok_rows + jnp.arange(tok_rows, dtype=jnp.int32)
    channel = head_place * quarter_width + jnp.arange(quarter_width, dtype=jnp.int32)
    features = (
        jax.nn.gelu(stem_sum + conv2_bias, approximate=False)
        + sinusoid(token_ids, channel, width_all)
    ).astype(jnp.bfloat16)
    quarter = lax.all_to_all(features, "head", split_axis=0, concat_axis=1, tiled=True)
    normed = layer_norm(quarter, norm_gain, norm_bias)
    widened_rows = lax.all_gather(qkv_weight, "head", axis=1, tiled=True)
    qkv_part = project_rows(normed, lax.all_gather(widened_rows, "seq", axis=0, tiled=True))
    return lax.all_to_all(
        qkv_part.astype(jnp.bfloat16), "head", split_axis=1, concat_axis=0, tiled=True
    )


MESH = pl.DeviceIdType.MESH
HALO = 16
ROWS = 128
W2_PIECES = (2, 0, 1, 5)
WQ_PIECES = (3, 4, 6)


def gelu(v):
    return 0.5 * v * (1.0 + lax.erf(v * math.sqrt(0.5)))


def fused_kernel(
    dims, seg_ref, b1_ref, b2_ref, gain_ref, shift_ref, mel_ref, w1_ref, w2_ref, wq_ref,
    out_ref, vec_ref, seg_own, seg_all, tail_send, tail_recv, fr, frp, halo_prev, halo_next, ebuf, obuf, x_even, x_odd,
    w1h, b1h, f_mid, f_odd, w2g, wqg, rest, restg, restq, restqg, acc0, accp, psend, precv, place,
    stem, gperm, nrm, seg_s, seg_r, tail_s, tail_r, fr_s, fr_r, halo_s, halo_r,
    w_s, w_r, loc, p_s, p_r, st_s, st_r,
):
    n, depth, width_all, quarter = dims
    nz = n // 2
    toks = fr.shape[1]
    frames_dev = 2 * toks
    plane = 2 * toks
    half_width = width_all // 2
    chunks = toks // ROWS
    me = lax.axis_index("seq")
    h = lax.axis_index("head")
    z, y = me // 2, me % 2
    partner = z * 2 + (1 - y)
    f32, bf16 = jnp.float32, jnp.bfloat16
    core = h % 2
    core_peer = (h // 2) * 2 + (1 - core)
    x_peer = lax.rem(h + 2, 4)
    far = lax.rem(core_peer + 2, 4)
    pending = []

    def remote(src, dst, ss, rs, axis, peer):
        return pltpu.make_async_remote_copy(
            src_ref=src, dst_ref=dst, send_sem=ss, recv_sem=rs,
            device_id={axis: peer}, device_id_type=MESH,
        )

    def start(cond, copy):
        if cond is None:
            copy.start()
        else:
            pl.when(cond)(copy.start)
        pending.append((cond, copy))

    def both(a, b):
        if a is None:
            return b
        return a if b is None else jnp.logical_and(a, b)

    barrier = pltpu.get_barrier_semaphore()
    for p in range(1, n):
        pl.semaphore_signal(
            barrier, inc=1, device_id={"seq": lax.rem(me + p, n)}, device_id_type=MESH
        )
    for p in range(1, 4):
        pl.semaphore_signal(
            barrier, inc=1, device_id={"head": lax.rem(h + p, 4)}, device_id_type=MESH
        )
    pl.semaphore_wait(barrier, n - 1 + 3)

    own_count = seg_ref[0]
    for i in range(1, seg_ref.shape[0]):
        own_count = own_count + seg_ref[i]
    seg_own[...] = jnp.full(seg_own.shape, own_count, jnp.int32)
    for p in range(1, n):
        dst = lax.rem(me + p, n)
        start(None, remote(seg_own, seg_all.at[me], seg_s.at[p], seg_r.at[me], "seq", dst))

    half = depth // 2
    out_cols = wqg.shape[1]
    main2, main_q = quarter - 64, out_cols - 64
    head_rows = 2 * depth - 64
    first_q = head_rows - depth
    lanes2, lanes_q = pl.ds(0, main2), pl.ds(0, main_q)
    rest_base = 4 * head_rows

    def row_first(s):
        return (s // 2) * head_rows + (s % 2) * depth

    def row_last(s):
        even = (s // 2) * head_rows + first_q
        odd = rest_base + (s // 2) * 64
        return (1 - s % 2) * even + (s % 2) * odd

    def gathered(p, s):
        if p < 3:
            return w2g.at[pl.ds(pl.multiple_of(p * half_width + (s // 2) * depth, 32), depth), lanes2]
        if p == 5:
            return restg.at[s // 2]
        if p == 6:
            return restqg.at[s]
        if p == 3:
            return wqg.at[pl.ds(pl.multiple_of(row_first(s), 32), first_q), lanes_q]
        return wqg.at[pl.ds(pl.multiple_of(row_last(s), 32), 64), lanes_q]

    def own(p):
        if p < 3:
            return w2_ref.at[p, :, lanes2]
        if p == 5:
            return rest
        if p == 6:
            return restq
        return wq_ref.at[pl.ds(0, first_q) if p == 3 else pl.ds(first_q, 64), lanes_q]

    has_up, has_down = z < nz - 1, z > 0

    def push(cond, p, s, way, mine=False):
        peer = (lax.rem(me + 2, n), lax.rem(me + n - 2, n), partner)[way]
        src = own(p) if mine else gathered(p, s)
        start(cond, remote(src, gathered(p, s), w_s.at[p, s, way], w_r.at[p, s], "seq", peer))

    def arrive(cond, p, s):
        copy = remote(gathered(p, s), gathered(p, s), w_s.at[p, s, 0], w_r.at[p, s], "seq", partner)
        if cond is None:
            copy.wait_recv()
        else:
            pl.when(cond)(copy.wait_recv)

    def own_along_z(p):
        push(has_up, p, me, 0, True)
        push(has_down, p, me, 1, True)

    def own_local(p):
        return pltpu.make_async_copy(own(p), gathered(p, me), loc.at[p])

    def source(k, way):
        valid = z - k >= 0 if way == 0 else z + k <= nz - 1
        onward = has_up if way == 0 else has_down
        s = lax.rem(me + (-2 * k if way == 0 else 2 * k) + 2 * n, n)
        return valid, onward, s

    def relay(p, k):
        for way in (0, 1):
            valid, onward, s = source(k, way)
            arrive(valid, p, s)
            push(both(valid, onward), p, s, way)

    middle = both(has_up, has_down)
    edge = jnp.logical_not(middle)

    def arrivals(p, k, where):
        for way in (0, 1):
            valid, _, s = source(k, way)
            arrive(both(valid, where), p, s)

    def onward_z(p, k):
        for way in (0, 1):
            valid, onward, s = source(k, way)
            push(both(valid, onward), p, s, way)

    def across_y(p, k, where, early=None):
        for way in (0, 1):
            valid, _, s = source(k, way)
            cond = both(valid, where)
            if early is not None:
                cond = both(cond, z % 2 == (1 - way if early else way))
            push(cond, p, s, 2)

    for p in WQ_PIECES:
        if p == 6:
            restq[:, 0:64] = wq_ref[0:half, main_q:]
            restq[:, 64:128] = wq_ref[half:, main_q:]
        if p == 4:
            continue
        push(None, p, me, 2, True)
        own_along_z(p)
    rest[0:depth, 0:64] = w2_ref[0, :, main2:]
    rest[0:depth, 64:128] = w2_ref[1, :, main2:]
    rest[depth:, 0:64] = w2_ref[2, 0:half, main2:]
    rest[depth:, 64:128] = w2_ref[2, half:, main2:]
    for p in W2_PIECES + WQ_PIECES:
        own_local(p).start()

    for row, ref in enumerate((b1_ref, gain_ref, shift_ref, b2_ref)):
        size = ref.shape[0]
        vec_ref[row : row + 1, 0:size] = ref[...].reshape(1, size)

    total = jnp.zeros((8, 128), jnp.int32)
    for p in range(1, n):
        src = lax.rem(me + n - p, n)
        remote(seg_own, seg_all.at[src], seg_s.at[p], seg_r.at[src], "seq", src).wait_recv()
        total = total + jnp.where(src < me, seg_all[src], 0)
    moved = total[0:1, 0:1] - me * frames_dev

    rows = ROWS

    def shifted(first, parity, depth_rows):
        frame = 2 * (first + lax.broadcasted_iota(jnp.int32, (rows, depth_rows), 0)) + parity
        column = lax.broadcasted_iota(jnp.int32, (rows, depth_rows), 1)
        pick = jnp.where(frame - column == moved, 1.0, 0.0).astype(bf16)
        return jnp.dot(pick, mel_ref[:depth_rows, :], preferred_element_type=f32)

    def tail_step(i, c):
        at = pl.multiple_of(i * rows, rows)
        tail_send[pl.ds(at, rows), :] = shifted(toks + at, core, 2 * frames_dev).astype(bf16)
        return c

    lax.fori_loop(0, toks // rows, tail_step, 0)
    tail = remote(tail_send, tail_recv.at[core], tail_s.at[0], tail_r.at[core],
                  "seq", lax.rem(me + 1, n))
    start(me < n - 1, tail)
    push(None, 4, me, 2, True)
    own_along_z(4)
    for p in W2_PIECES:
        own_along_z(p)
    ebuf[0:HALO, :] = jnp.zeros((HALO, 128), f32)
    obuf[0:HALO, :] = jnp.zeros((HALO, 128), f32)
    ebuf[HALO + plane :, :] = jnp.zeros((HALO, 128), f32)

    base = pl.multiple_of(HALO + y * toks, 16)
    other = pl.multiple_of(HALO + (1 - y) * toks, 16)
    for parity, buf in ((0, ebuf), (1, obuf)):
        def own_step(i, c):
            at = pl.multiple_of(i * rows, rows)
            buf[pl.ds(base + at, rows), :] = shifted(at, parity, frames_dev)
            return c
        lax.fori_loop(0, toks // rows, own_step, 0)
    for p in W2_PIECES[:2]:
        relay(p, 1)

    pl.when(me > 0)(tail.wait_recv)
    start(me > 0, remote(tail_recv.at[core], tail_recv.at[core], tail_s.at[1], tail_r.at[core],
                         "head", core_peer))
    pl.when(me > 0)(remote(
        tail_recv.at[1 - core], tail_recv.at[1 - core], tail_s.at[1], tail_r.at[1 - core],
        "head", core_peer).wait_recv)
    for parity, buf in ((0, ebuf), (1, obuf)):
        frame = 2 * lax.broadcasted_iota(jnp.int32, (toks, 128), 0) + parity
        joined = jnp.where(
            frame < moved, tail_recv[parity].astype(f32), buf[pl.ds(base, toks), :])
        buf[pl.ds(base, toks), :] = joined
        fr[parity] = joined.astype(bf16)

    start(None, remote(fr.at[core], frp.at[core], fr_s.at[0], fr_r.at[core], "seq", partner))
    upper, lower = both(y == 1, has_up), both(y == 0, has_down)
    one, two = lax.rem(me + 1, n), lax.rem(me + 2, n)
    back, back2 = lax.rem(me + n - 1, n), lax.rem(me + n - 2, n)
    tail_rows, head_part = pl.ds(toks - HALO, HALO), pl.ds(0, HALO)
    for i, peer in enumerate((one, two)):
        for parity in (0, 1):
            start(upper, remote(fr.at[parity, tail_rows, :], halo_prev.at[parity],
                                halo_s.at[2 * i + parity], halo_r.at[parity], "seq", peer))
    for i, peer in enumerate((back, back2)):
        start(lower, remote(fr.at[0, head_part, :], halo_next,
                            halo_s.at[4 + i], halo_r.at[2], "seq", peer))
    for p in W2_PIECES[2:]:
        relay(p, 1)
    for p in WQ_PIECES:
        arrivals(p, 1, None)
        across_y(p, 1, None, True)

    for yy in (0, 1):
        @pl.when(y == yy)
        def _():
            for q in range(nz):
                dst = slice(q * depth, (q + 1) * depth)
                src = slice((2 * q + yy) * depth, (2 * q + yy + 1) * depth)
                w1h[:, dst] = w1_ref[:, src]
                b1h[0:1, dst] = vec_ref[0:1, src]
    for j in range(4):
        a, b = j * quarter, j * quarter + main2
        for r in (0, 1):
            gperm[r : r + 1, j * main2 : (j + 1) * main2] = vec_ref[1 + r : 2 + r, a:b]
            gperm[r : r + 1, rest_base + j * 64 : rest_base + (j + 1) * 64] = (
                vec_ref[1 + r : 2 + r, b : b + 64])

    first_token = lax.rem(me * toks, CONTEXT)
    lane = lax.broadcasted_iota(jnp.int32, (1, main2), 1)
    first_channel = lax.rem(h * quarter, half_width)

    def rate_of(channel):
        return jnp.exp(-(LOG_SCALE / (half_width - 1)) * (channel + first_channel).astype(f32))

    rate_main, rate_rest = rate_of(lane), rate_of(main2 + lax.rem(lane, 64))
    packed = ROWS + ROWS // 4

    def fill_place(wave):
        def step(i, c):
            token = first_token + i * ROWS + lax.broadcasted_iota(jnp.int32, (ROWS, 1), 0)
            token = jnp.where(token >= CONTEXT, token - CONTEXT, token)
            place[i, 0:ROWS, :] = wave(token.astype(f32) * rate_main)
            shape = (ROWS // 4, main2)
            token = (first_token + i * ROWS + lax.broadcasted_iota(jnp.int32, shape, 0)
                     + (ROWS // 4) * (lax.broadcasted_iota(jnp.int32, shape, 1) // 64))
            token = jnp.where(token >= CONTEXT, token - CONTEXT, token)
            place[i, ROWS:packed, :] = wave(token.astype(f32) * rate_rest)
            return c
        lax.fori_loop(0, chunks, step, 0)

    pl.when(h < 2)(lambda: fill_place(jnp.sin))
    pl.when(h >= 2)(lambda: fill_place(jnp.cos))

    for p in W2_PIECES[:2]:
        relay(p, 2)

    remote(fr.at[core], frp.at[core], fr_s.at[0], fr_r.at[core], "seq", partner).wait_recv()
    start(None, remote(frp.at[core], frp.at[core], fr_s.at[1], fr_r.at[core], "head", core_peer))
    remote(frp.at[1 - core], frp.at[1 - core], fr_s.at[1], fr_r.at[1 - core],
           "head", core_peer).wait_recv()
    ebuf[pl.ds(other, toks), :] = frp[0].astype(f32)
    obuf[pl.ds(other, toks), :] = frp[1].astype(f32)
    x_even[:, 0:128] = obuf[HALO - 1 : HALO - 1 + plane, :].astype(bf16)
    x_even[:, 128:256] = ebuf[HALO : HALO + plane, :].astype(bf16)
    x_even[:, 256:384] = obuf[HALO : HALO + plane, :].astype(bf16)
    x_odd[HALO:, 0:128] = ebuf[HALO : HALO + plane, :].astype(bf16)
    x_odd[HALO:, 128:256] = obuf[HALO : HALO + plane, :].astype(bf16)
    x_odd[HALO:, 256:384] = ebuf[HALO + 1 : HALO + plane + 1, :].astype(bf16)

    tiles = [(a, min(a + 256, half_width)) for a in range(0, half_width, 256)]

    def first_conv(inputs, a, b):
        acc = jnp.dot(inputs, w1h[:, a:b], preferred_element_type=f32)
        return gelu(acc + b1h[0:1, a:b]).astype(bf16)

    def even_step(i, c):
        at = pl.ds(pl.multiple_of(i * toks, 16), toks)
        for a, b in tiles:
            f_mid[at, a:b] = first_conv(x_even[at, :], a, b)
        return c

    def odd_step(i, c):
        at = pl.multiple_of(i * toks, 16)
        for a, b in tiles:
            value = first_conv(x_odd[pl.ds(HALO + at, toks), :], a, b)
            f_mid[pl.ds(at, toks), half_width + a : half_width + b] = value
            f_odd[pl.ds(HALO + at, toks), a:b] = value
        return c

    lax.fori_loop(0, 2, even_step, 0)
    for p in W2_PIECES[2:]:
        relay(p, 2)
    for p in WQ_PIECES:
        onward_z(p, 1)
    lax.fori_loop(0, 2, odd_step, 0)
    for i in (0, 1):
        pl.when(has_down)(remote(halo_prev.at[i], halo_prev.at[i], halo_s.at[i], halo_r.at[i],
                                 "seq", partner).wait_recv)
    pl.when(has_up)(remote(halo_next, halo_next, halo_s.at[4], halo_r.at[2],
                           "seq", partner).wait_recv)
    ebuf[0:HALO, :] = jnp.where(z > 0, halo_prev[0].astype(f32), 0.0)
    obuf[0:HALO, :] = jnp.where(z > 0, halo_prev[1].astype(f32), 0.0)
    ebuf[HALO + plane :, :] = jnp.where(z < nz - 1, halo_next[...].astype(f32), 0.0)
    x_even[0:HALO, 0:128] = obuf[HALO - 1 : 2 * HALO - 1, :].astype(bf16)
    x_odd[0:HALO, 0:128] = ebuf[0:HALO, :].astype(bf16)
    x_odd[0:HALO, 128:256] = obuf[0:HALO, :].astype(bf16)
    x_odd[0:HALO, 256:384] = ebuf[1 : HALO + 1, :].astype(bf16)
    x_odd[plane:, 256:384] = ebuf[plane + 1 : HALO + plane + 1, :].astype(bf16)
    for a, b in tiles:
        early = first_conv(x_odd[0:HALO, :], a, b)
        f_odd[0:HALO, a:b] = jnp.where(z > 0, early.astype(f32), 0.0).astype(bf16)
        f_mid[0:HALO, a:b] = first_conv(x_even[0:HALO, :], a, b)
        late = first_conv(x_odd[plane:, :], a, b)
        f_odd[plane:, a:b] = late
        f_mid[plane - HALO :, half_width + a : half_width + b] = late

    for p in W2_PIECES:
        relay(p, 3)
    for p in W2_PIECES + WQ_PIECES:
        own_local(p).wait()
    for q in range(nz):
        for tap in (0, 1):
            at = tap * half_width + q * depth
            w2g[at : at + depth, main2:] = restg[q, 0:depth, 64 * tap : 64 * tap + 64]
        at = 2 * half_width + q * depth
        w2g[at : at + half, main2:] = restg[q, depth:, 0:64]
        w2g[at + half : at + depth, main2:] = restg[q, depth:, 64:128]

    odd_rows = (HALO + toks) // 3

    def partial_sums(slab, store):
        def tap_zero(i, c):
            at = pl.multiple_of(i * odd_rows, 16)
            acc0[pl.ds(at, odd_rows), :] = jnp.dot(
                f_odd[pl.ds(pl.multiple_of(slab * toks + at, 16), odd_rows), :],
                w2g[0:half_width, :], preferred_element_type=f32)
            return c

        lax.fori_loop(0, 3, tap_zero, 0)
        for i in range(chunks):
            at = pl.multiple_of(slab * toks + i * ROWS, ROWS)
            acc = jnp.dot(f_mid[pl.ds(at, ROWS), :], w2g[half_width:, :], preferred_element_type=f32)
            acc = acc + acc0[HALO - 1 + i * ROWS : HALO - 1 + (i + 1) * ROWS, :]
            store(i, acc)

    def store_packed(ref, i, acc):
        acc = acc.astype(ref.dtype)
        ref[i, 0:ROWS, :] = acc[:, 0:main2]
        step = ROWS // 4
        for b in range(4):
            ref[i, ROWS:packed, 64 * b : 64 * b + 64] = acc[b * step : (b + 1) * step, main2:]

    def send_partial(i, acc):
        store_packed(psend, i, acc)
        start(None, remote(psend.at[i], precv.at[i], p_s.at[i], p_r.at[i], "seq", partner))

    partial_sums(1 - y, send_partial)
    for p in WQ_PIECES:
        across_y(p, 1, middle, False)
    for p in WQ_PIECES:
        arrivals(p, 2, middle)
        onward_z(p, 2)
        across_y(p, 2, middle)
    partial_sums(y, lambda i, acc: store_packed(accp, i, acc))

    bias_main = vec_ref[3:4, 0:main2]
    bias_rest = jnp.concatenate([vec_ref[3:4, main2:quarter]] * 4, axis=1)
    for i in range(chunks):
        if i == chunks - 1:
            for p in WQ_PIECES:
                arrivals(p, 2, edge)
                across_y(p, 2, edge)
        remote(psend.at[i], precv.at[i], p_s.at[i], p_r.at[i], "seq", partner).wait_recv()
        for part, bias in ((slice(0, ROWS), bias_main), (slice(ROWS, packed), bias_rest)):
            value = accp[i, part, :] + precv[i, part, :].astype(f32) + bias
            stem[h, i, part, :] = (gelu(value) + place[i, part, :]).astype(bf16)
        mine = stem.at[h, i]
        start(None, remote(mine, mine, st_s.at[0, i], st_r.at[0, i], "head", x_peer))
        start(None, remote(mine, mine, st_s.at[1, i], st_r.at[1, i], "head", core_peer))

    for i in range(chunks):
        got = stem.at[x_peer, i]
        remote(got, got, st_s.at[0, i], st_r.at[0, i], "head", x_peer).wait_recv()
        start(None, remote(got, got, st_s.at[2, i], st_r.at[2, i], "head", core_peer))
    for i in range(chunks):
        got = stem.at[core_peer, i]
        remote(got, got, st_s.at[1, i], st_r.at[1, i], "head", core_peer).wait_recv()
        got = stem.at[far, i]
        remote(got, got, st_s.at[2, i], st_r.at[2, i], "head", core_peer).wait_recv()

    def normalise(i, c):
        step = ROWS // 4
        parts = [stem[j, i, 0:ROWS, :].astype(f32) for j in range(4)]
        tails = [stem[j, i, ROWS:packed, :].astype(f32) for j in range(4)]
        parts.append(jnp.concatenate(
            [jnp.concatenate([t[:, 64 * b : 64 * b + 64] for t in tails], axis=1) for b in range(4)],
            axis=0))
        mean = jnp.sum(sum(parts), axis=1, keepdims=True) / width_all
        parts = [v - mean for v in parts]
        var = jnp.sum(sum(v * v for v in parts), axis=1, keepdims=True) / width_all
        scale = lax.rsqrt(var + 1e-05)
        at = pl.ds(pl.multiple_of(i * ROWS, ROWS), ROWS)
        for j, v in enumerate(parts):
            lanes = slice(j * main2, (j + 1) * main2)
            nrm[at, lanes] = (v * scale * gperm[0:1, lanes] + gperm[1:2, lanes]).astype(bf16)
        return c

    for p in WQ_PIECES[:1]:
        arrivals(p, 3, None)
        across_y(p, 3, None)
    lax.fori_loop(0, chunks, normalise, 0)
    for p in WQ_PIECES[1:]:
        arrivals(p, 3, None)
        across_y(p, 3, None)
    for p in WQ_PIECES:
        for q in range(nz):
            arrive(None, p, 2 * q + (1 - y))
    for s in range(n):
        lo, hi = row_first(s), row_last(s)
        wqg[lo : lo + half, main_q:] = restqg[s, :, 0:64]
        wqg[lo + half : lo + first_q, main_q:] = restqg[s, 0 : first_q - half, 64:128]
        wqg[hi : hi + 64, main_q:] = restqg[s, first_q - half :, 64:128]

    def project(i, c):
        at = pl.ds(pl.multiple_of(i * 256, 256), 256)
        for a in range(0, out_cols, 256):
            b = min(a + 256, out_cols)
            out_ref[at, a:b] = jnp.dot(
                nrm[at, :], wqg[:, a:b], preferred_element_type=f32).astype(bf16)
        return c

    lax.fori_loop(0, toks // 256, project, 0)

    for cond, copy in pending:
        if cond is None:
            copy.wait_send()
        else:
            pl.when(cond)(copy.wait_send)


def fused_device(
    n, mel_buffer, segment_frames, conv1_weight, conv1_bias, conv2_weight, conv2_bias,
    norm_gain, norm_bias, qkv_weight,
):
    toks = mel_buffer.shape[0] // 4
    taps, mels, width_all = conv1_weight.shape
    depth, quarter = conv2_weight.shape[1:]
    out_cols = qkv_weight.shape[1]
    bf16, f32 = jnp.bfloat16, jnp.float32
    vmem = pl.BlockSpec(memory_space=pltpu.VMEM)
    dma = pltpu.SemaphoreType.DMA
    plane, inner = 2 * toks, width_all // 2
    chunks, packed, main2 = toks // ROWS, ROWS + ROWS // 4, quarter - 64
    return pl.pallas_call(
        functools.partial(fused_kernel, (n, depth, width_all, quarter)),
        out_shape=jax.ShapeDtypeStruct((toks, out_cols), bf16),
        in_specs=[pl.BlockSpec(memory_space=pltpu.SMEM)] + [vmem] * 8,
        out_specs=vmem,
        scratch_shapes=[
            pltpu.VMEM((8, width_all), f32),
            pltpu.VMEM((8, 128), jnp.int32),
            pltpu.VMEM((n, 8, 128), jnp.int32),
            pltpu.VMEM((toks, 128), bf16),
            pltpu.VMEM((2, toks, 128), bf16),
            pltpu.VMEM((2, toks, 128), bf16),
            pltpu.VMEM((2, toks, 128), bf16),
            pltpu.VMEM((2, HALO, 128), bf16),
            pltpu.VMEM((HALO, 128), bf16),
            pltpu.VMEM((plane + 2 * HALO, 128), f32),
            pltpu.VMEM((plane + 2 * HALO, 128), f32),
            pltpu.VMEM((plane, 384), bf16),
            pltpu.VMEM((plane + HALO, 384), bf16),
            pltpu.VMEM((taps * mels, inner), bf16),
            pltpu.VMEM((8, inner), f32),
            pltpu.VMEM((plane, width_all), bf16),
            pltpu.VMEM((plane + HALO, inner), bf16),
            pltpu.VMEM((3 * inner, quarter), bf16),
            pltpu.VMEM((width_all, out_cols), bf16),
            pltpu.VMEM((3 * depth // 2, 128), bf16),
            pltpu.VMEM((n // 2, 3 * depth // 2, 128), bf16),
            pltpu.VMEM((depth // 2, 128), bf16),
            pltpu.VMEM((n, depth // 2, 128), bf16),
            pltpu.VMEM((toks + HALO, quarter), f32),
            pltpu.VMEM((chunks, packed, main2), f32),
            pltpu.VMEM((chunks, packed, main2), bf16),
            pltpu.VMEM((chunks, packed, main2), bf16),
            pltpu.VMEM((chunks, packed, main2), f32),
            pltpu.VMEM((4, chunks, packed, main2), bf16),
            pltpu.VMEM((8, width_all), f32),
            pltpu.VMEM((toks, width_all), bf16),
            dma((n,)), dma((n,)), dma((2,)), dma((2,)), dma((2,)), dma((2,)), dma((6,)), dma((3,)),
            dma((7, n, 3)), dma((7, n)), dma((7,)), dma((chunks,)), dma((chunks,)),
            dma((3, chunks)), dma((3, chunks)),
        ],
        compiler_params=pltpu.CompilerParams(
            collective_id=0, has_side_effects=True, vmem_limit_bytes=60 * 1024 * 1024
        ),
    )(
        segment_frames, conv1_bias, conv2_bias, norm_gain, norm_bias, mel_buffer,
        conv1_weight.reshape(taps * mels, width_all), conv2_weight, qkv_weight,
    )


def solution(mesh):
    n_seq, n_head = mesh.shape["seq"], mesh.shape["head"]

    def local(*args):
        depth, quarter = args[4].shape[1:]
        fits = n_head == 4 and n_seq == 8 and depth == 160 and quarter == 320
        if fits and args[0].shape[0] == 2048:
            return fused_device(n_seq, *args)
        return per_device(*args)

    in_specs = (
        P("seq", None),
        P("seq"),
        P(),
        P(),
        P(None, "seq", "head"),
        P("head"),
        P(),
        P(),
        P("seq", "head"),
    )
    out_specs = P("seq", "head")
    return jax.shard_map(
        local, mesh=mesh, in_specs=in_specs, out_specs=out_specs, check_vma=False
    )
```
